32 devices in a mesh: groups: 2 (over y), row: 8 (over z, x), col: 2 (over core).
Axes of the slice: x: 2, y: 2, z: 4, core: 2. Of those that a mesh axis runs over, the one named last changes fastest.
Arguments:
- inputs: bfloat16 [32, 8192], P(('groups', 'row'), 'col'), parts along dimension 0, may hold values from -6 to 6
- out_grads: bfloat16 [32, 8192], P(('groups', 'row'), 'col'), parts along dimension 0, may hold values from -6 to 6
- w_gate: bfloat16 [8192, 24576], P('col', 'row'), may hold values from -0.0625 to 0.0625
- w_up: bfloat16 [8192, 24576], P('col', 'row'), may hold values from -0.0625 to 0.0625
- w_down: bfloat16 [24576, 8192], P('row', 'col'), may hold values from -0.0390625 to 0.0390625
Outputs:
- attribution: float32 [32, 8192], P(('groups', 'row'), 'col'), parts along dimension 0
The draws below stay inside these ranges and needn't reach their ends.
There are 2 independent parts, one for each index of `groups`. The reference program is written for one: setup_inputs(seed, part) draws one part's arguments, and reference() takes and returns one part's arrays. A program takes and returns all parts, laid end to end along the dimension named above; an argument that names none is the same for every part. Nothing has to cross between parts.
All inputs are finite; a program needn't handle non-finite values.
Results may differ from the reference program's by a relative error of at most 0.0029.
Values may be sent and summed in bfloat16 or wider, within the bound.
A program may use at most 192 MiB of HBM per device.

```python
import jax
import jax.numpy as jnp
from jax import lax

D = 8192
FF = 24576
TOKENS = 16


def levels(own_key, extent, shards, low, high):
    factor_of = 1.0
    for axis_at, parts in shards:
        draws = jax.random.uniform(jax.random.fold_in(jax.random.fold_in(own_key, 6), axis_at), (parts,), jnp.float32, low / len(shards), high / len(shards))
        factor_of = factor_of * jnp.repeat(jnp.exp(draws), extent[axis_at] // parts).reshape((-1,) + (1,) * (len(extent) - 1 - axis_at))
    return factor_of


def centred(key, shape, width, limit, split=(), dtype=jnp.bfloat16):
    level = levels(key, shape, split, -0.22, 0.18) if split else 1.0
    array = jax.random.normal(key, shape, jnp.float32) * width * level
    return jnp.minimum(jnp.maximum(array, -limit), limit).astype(dtype)


def setup_inputs(seed: int = 0, part: int = 0) -> dict:
    splits = jax.random.split(jax.random.key(seed), 6)
    part_keys = jax.random.split(jax.random.fold_in(splits[5], part), 6)
    inputs = centred(part_keys[0], (TOKENS, D), 1.0, 6.0, ((0, 8), (1, 2)))
    out_grads = centred(part_keys[1], (TOKENS, D), 1.0, 6.0, ((0, 8), (1, 2)))
    w_gate = centred(splits[2], (D, FF), D ** -0.5, 0.0625, ((0, 2), (1, 8)))
    w_up = centred(splits[3], (D, FF), D ** -0.5, 0.0625, ((0, 2), (1, 8)))
    w_down = centred(splits[4], (FF, D), FF ** -0.5, 0.0390625, ((0, 8), (1, 2)))
    return dict(inputs=inputs, out_grads=out_grads, w_gate=w_gate, w_up=w_up, w_down=w_down)


def reference(inputs, out_grads, w_gate, w_up, w_down):
    gated = jnp.dot(inputs, w_gate, preferred_element_type=jnp.float32)
    upward = jnp.dot(inputs, w_up, preferred_element_type=jnp.float32)
    backward = lax.dot_general(out_grads, w_down, (((1,), (1,)), ((), ())), preferred_element_type=jnp.float32)
    sigma = jax.nn.sigmoid(gated)
    grad_gate = (backward * upward * sigma * (1.0 + gated * (1.0 - sigma))).astype(jnp.bfloat16)
    grad_up = (backward * gated * sigma).astype(jnp.bfloat16)
    grad_input = lax.dot_general(grad_gate, w_gate, (((1,), (1,)), ((), ())), preferred_element_type=jnp.float32)
    grad_input = grad_input + lax.dot_general(grad_up, w_up, (((1,), (1,)), ((), ())), preferred_element_type=jnp.float32)
    return inputs.astype(jnp.float32) * grad_input
```

```python
import functools

import jax
import jax.numpy as jnp
from jax import lax
from jax.experimental import pallas as pl
from jax.experimental.pallas import tpu as pltpu
from jax.sharding import PartitionSpec as P

MESH = pl.DeviceIdType.MESH
TILE = 256
NT = (((1,), (1,)), ((), ()))


def derivatives(sums):
    gated = sums[0]
    upward = sums[1]
    backward = sums[2]
    sigma = jax.nn.sigmoid(gated)
    grad_gate = (backward * upward * sigma * (1.0 + gated * (1.0 - sigma))).astype(jnp.bfloat16)
    grad_up = (backward * gated * sigma).astype(jnp.bfloat16)
    return jnp.stack([grad_gate, grad_up])


def per_device(inputs, out_grads, w_gate, w_up, w_down):
    stacked = jnp.stack([inputs, out_grads])
    piece = lax.all_gather(stacked, "row", axis=1, tiled=True)
    gated = jnp.dot(piece[0], w_gate, preferred_element_type=jnp.float32)
    upward = jnp.dot(piece[0], w_up, preferred_element_type=jnp.float32)
    backward = lax.dot_general(piece[1], w_down, NT, preferred_element_type=jnp.float32)
    partial_sums = jnp.stack([gated, upward, backward])
    summed = lax.psum(partial_sums, "col")
    derived = derivatives(summed)
    total = lax.dot_general(derived[0], w_gate, NT, preferred_element_type=jnp.float32)
    grad_input = lax.psum_scatter(
        total + lax.dot_general(derived[1], w_up, NT, preferred_element_type=jnp.float32),
        "row",
        scatter_dimension=0,
        tiled=True,
    )
    return inputs.astype(jnp.float32) * grad_input


def kernel(
    nz, tiles,
    in_hbm, og_hbm, wg_hbm, wu_hbm, wd_hbm, out_ref,
    wg, wu, wd, gx, gy, stage, xs, ys, part, peer, acc, own, s1, r1, mid, s2, r2,
    w_sem, l_sem, z_send, z_recv, p_send, p_recv, c_send, c_recv,
    a_send, a_recv, b_send, b_recv,
):
    tokens, feats = in_hbm.shape
    rows = nz * tokens
    half = tiles * TILE
    g = lax.axis_index("groups")
    r = lax.axis_index("row")
    c = lax.axis_index("col")
    x = lax.rem(r, 2)
    z = r // 2
    plane = g * 2 + x

    def z_dev(d):
        return {"row": lax.rem(z + d, nz) * 2 + x}

    def p_index(d):
        return lax.rem(plane + d, 4)

    def p_dev(d):
        q = lax.rem(plane + d, 4)
        return {"groups": q // 2, "row": z * 2 + lax.rem(q, 2)}

    def weight_copies(j):
        at = pl.multiple_of(g * half + j * TILE, TILE)
        return (
            pltpu.make_async_copy(wg_hbm.at[:, pl.ds(at, TILE)], wg.at[j], w_sem.at[0, j]),
            pltpu.make_async_copy(wu_hbm.at[:, pl.ds(at, TILE)], wu.at[j], w_sem.at[1, j]),
            pltpu.make_async_copy(wd_hbm.at[pl.ds(at, TILE), :], wd.at[j], w_sem.at[2, j]),
        )

    own_x = pltpu.make_async_copy(in_hbm, gx.at[plane, z], l_sem.at[0])
    own_y = pltpu.make_async_copy(og_hbm, gy.at[plane, z], l_sem.at[1])
    own_x.start()
    own_y.start()

    @pl.loop(0, tiles)
    def _(j):
        for copy in weight_copies(j):
            copy.start()

    barrier = pltpu.get_barrier_semaphore()
    for d in range(1, nz):
        pl.semaphore_signal(barrier, inc=1, device_id=z_dev(d), device_id_type=MESH)
    for d in range(1, 4):
        pl.semaphore_signal(barrier, inc=1, device_id=p_dev(d), device_id_type=MESH)
    pl.semaphore_signal(barrier, inc=1, device_id={"col": 1 - c}, device_id_type=MESH)
    pl.semaphore_wait(barrier, nz + 3)

    sources = ((in_hbm, gx), (og_hbm, gy))
    z_copies = [
        [
            pltpu.make_async_remote_copy(
                src_ref=src, dst_ref=buf.at[plane, z],
                send_sem=z_send.at[a, d - 1], recv_sem=z_recv.at[a, d - 1],
                device_id=z_dev(d), device_id_type=MESH,
            )
            for d in range(1, nz)
        ]
        for a, (src, buf) in enumerate(sources)
    ]
    p_copies = [
        [
            pltpu.make_async_remote_copy(
                src_ref=buf.at[plane], dst_ref=buf.at[plane],
                send_sem=p_send.at[a, d - 1], recv_sem=p_recv.at[a, d - 1],
                device_id=p_dev(d), device_id_type=MESH,
            )
            for d in range(1, 4)
        ]
        for a, (_, buf) in enumerate(sources)
    ]
    for a in range(2):
        for copy in z_copies[a]:
            copy.start()
    for a, local in enumerate((own_x, own_y)):
        local.wait()
        for copy in z_copies[a]:
            copy.wait_recv()
        for copy in p_copies[a]:
            copy.start()

    def arrange(a, buf, dst):
        for copy in p_copies[a]:
            copy.wait_recv()
        for q in range(4):
            for k in range(nz):
                at = q * rows + k * tokens
                stage[at:at + tokens, :] = buf[q, k].astype(jnp.float32)
        dst[...] = stage[...].astype(jnp.bfloat16)

    arrange(0, gx, xs)
    arrange(1, gy, ys)
    acc[...] = jnp.zeros_like(acc)

    def exchange(j):
        return pltpu.make_async_remote_copy(
            src_ref=part.at[j], dst_ref=peer.at[j],
            send_sem=c_send.at[j], recv_sem=c_recv.at[j],
            device_id={"col": 1 - c}, device_id_type=MESH,
        )

    def forward(j):
        gate, up, down = weight_copies(j)
        gate.wait()
        part[j, 0] = jnp.dot(xs[...], wg[j], preferred_element_type=jnp.float32)
        up.wait()
        part[j, 1] = jnp.dot(xs[...], wu[j], preferred_element_type=jnp.float32)
        down.wait()
        part[j, 2] = lax.dot_general(ys[...], wd[j], NT, preferred_element_type=jnp.float32)
        exchange(j).start()

    def finish(j):
        exchange(j).wait_recv()
        gated = part[j, 0] + peer[j, 0]
        upward = part[j, 1] + peer[j, 1]
        backward = part[j, 2] + peer[j, 2]
        sigma = 1.0 / (1.0 + jnp.exp(-gated))
        gate = (backward * upward * sigma * (1.0 + gated * (1.0 - sigma))).astype(jnp.bfloat16)
        up = (backward * gated * sigma).astype(jnp.bfloat16)
        acc[...] += lax.dot_general(
            gate, wg[j], NT, preferred_element_type=jnp.float32
        ) + lax.dot_general(up, wu[j], NT, preferred_element_type=jnp.float32)

    @pl.loop(0, tiles + 1)
    def _(j):
        @pl.when(j < tiles)
        def _():
            forward(j)

        @pl.when(j > 0)
        def _():
            finish(j - 1)

    for q in range(4):
        s1[q] = acc[q * rows:(q + 1) * rows, :].astype(jnp.bfloat16)
    a_copies = [
        pltpu.make_async_remote_copy(
            src_ref=s1.at[p_index(d)], dst_ref=r1.at[d - 1],
            send_sem=a_send.at[d - 1], recv_sem=a_recv.at[d - 1],
            device_id=p_dev(d), device_id_type=MESH,
        )
        for d in range(1, 4)
    ]
    for copy in a_copies:
        copy.start()
    own[...] = acc[pl.ds(pl.multiple_of(plane * rows, rows), rows), :]
    for copy in a_copies:
        copy.wait_recv()
    own[...] = own[...] + r1[0].astype(jnp.float32) + r1[1].astype(jnp.float32) + r1[2].astype(jnp.float32)
    for k in range(nz):
        mid[k] = own[k * tokens:(k + 1) * tokens, :]
        s2[k] = mid[k].astype(jnp.bfloat16)
    b_copies = [
        pltpu.make_async_remote_copy(
            src_ref=s2.at[lax.rem(z + d, nz)], dst_ref=r2.at[d - 1],
            send_sem=b_send.at[d - 1], recv_sem=b_recv.at[d - 1],
            device_id=z_dev(d), device_id_type=MESH,
        )
        for d in range(1, nz)
    ]
    for copy in b_copies:
        copy.start()
    total = mid[z]
    for d in range(1, nz):
        b_copies[d - 1].wait_recv()
        total = total + r2[d - 1].astype(jnp.float32)
    out_ref[...] = gx[plane, z].astype(jnp.float32) * total

    for copies in z_copies + p_copies + [a_copies, b_copies]:
        for copy in copies:
            copy.wait_send()

    @pl.loop(0, tiles)
    def _(j):
        exchange(j).wait_send()


def shared(nz, inputs, out_grads, w_gate, w_up, w_down):
    tokens, feats = inputs.shape
    tiles = w_gate.shape[1] // (2 * TILE)
    rows = nz * tokens
    every = 4 * rows
    f32, bf16 = jnp.float32, jnp.bfloat16
    dma = pltpu.SemaphoreType.DMA
    return pl.pallas_call(
        functools.partial(kernel, nz, tiles),
        out_shape=jax.ShapeDtypeStruct((tokens, feats), f32),
        in_specs=[pl.BlockSpec(memory_space=pl.ANY)] * 5,
        out_specs=pl.BlockSpec(memory_space=pltpu.VMEM),
        scratch_shapes=[
            pltpu.VMEM((tiles, feats, TILE), bf16),
            pltpu.VMEM((tiles, feats, TILE), bf16),
            pltpu.VMEM((tiles, TILE, feats), bf16),
            pltpu.VMEM((4, nz, tokens, feats), bf16),
            pltpu.VMEM((4, nz, tokens, feats), bf16),
            pltpu.VMEM((every, feats), f32),
            pltpu.VMEM((every, feats), bf16),
            pltpu.VMEM((every, feats), bf16),
            pltpu.VMEM((tiles, 3, every, TILE), f32),
            pltpu.VMEM((tiles, 3, every, TILE), f32),
            pltpu.VMEM((every, feats), f32),
            pltpu.VMEM((rows, feats), f32),
            pltpu.VMEM((4, rows, feats), bf16),
            pltpu.VMEM((3, rows, feats), bf16),
            pltpu.VMEM((nz, tokens, feats), f32),
            pltpu.VMEM((nz, tokens, feats), bf16),
            pltpu.VMEM((nz - 1, tokens, feats), bf16),
            dma((3, tiles)), dma((2,)),
            dma((2, nz - 1)), dma((2, nz - 1)),
            dma((2, 3)), dma((2, 3)),
            dma((tiles,)), dma((tiles,)),
            dma((3,)), dma((3,)),
            dma((nz - 1,)), dma((nz - 1,)),
        ],
        compiler_params=pltpu.CompilerParams(
            collective_id=0, has_side_effects=True, vmem_limit_bytes=60 << 20
        ),
    )(inputs, out_grads, w_gate, w_up, w_down)


def solution(mesh):
    in_specs = (
        P(("groups", "row"), "col"),
        P(("groups", "row"), "col"),
        P("col", "row"),
        P("col", "row"),
        P("row", "col"),
    )
    out_specs = P(("groups", "row"), "col")
    groups, row, col = (mesh.shape[name] for name in ("groups", "row", "col"))

    def body(inputs, out_grads, w_gate, w_up, w_down):
        tokens, feats = inputs.shape
        nz = row // 2
        hidden = w_gate.shape[1]
        held = 3 * feats * hidden + 60 * groups * row * tokens * feats
        fits = (
            groups == 2 and col == 2 and row % 2 == 0 and nz > 1
            and hidden % (2 * TILE) == 0 and feats % TILE == 0
            and nz * tokens == 8 and held < (56 << 20)
        )
        plan = functools.partial(shared, nz) if fits else per_device
        return plan(inputs, out_grads, w_gate, w_up, w_down)

    return jax.shard_map(
        body, mesh=mesh, in_specs=in_specs, out_specs=out_specs, check_vma=False
    )
```

```python
import functools

import jax
import jax.numpy as jnp
from jax import lax
from jax.experimental import pallas as pl
from jax.experimental.pallas import tpu as pltpu
from jax.sharding import PartitionSpec as P

MESH = pl.DeviceIdType.MESH
TILE = 512
CHUNKS = 4
NT = (((1,), (1,)), ((), ()))


def derivatives(sums):
    gated = sums[0]
    upward = sums[1]
    backward = sums[2]
    sigma = jax.nn.sigmoid(gated)
    grad_gate = (backward * upward * sigma * (1.0 + gated * (1.0 - sigma))).astype(jnp.bfloat16)
    grad_up = (backward * gated * sigma).astype(jnp.bfloat16)
    return jnp.stack([grad_gate, grad_up])


def per_device(inputs, out_grads, w_gate, w_up, w_down):
    stacked = jnp.stack([inputs, out_grads])
    piece = lax.all_gather(stacked, "row", axis=1, tiled=True)
    gated = jnp.dot(piece[0], w_gate, preferred_element_type=jnp.float32)
    upward = jnp.dot(piece[0], w_up, preferred_element_type=jnp.float32)
    backward = lax.dot_general(piece[1], w_down, NT, preferred_element_type=jnp.float32)
    partial_sums = jnp.stack([gated, upward, backward])
    summed = lax.psum(partial_sums, "col")
    derived = derivatives(summed)
    total = lax.dot_general(derived[0], w_gate, NT, preferred_element_type=jnp.float32)
    grad_input = lax.psum_scatter(
        total + lax.dot_general(derived[1], w_up, NT, preferred_element_type=jnp.float32),
        "row",
        scatter_dimension=0,
        tiled=True,
    )
    return inputs.astype(jnp.float32) * grad_input


def kernel(
    nz, tiles,
    in_hbm, og_hbm, wg_hbm, wu_hbm, wd_hbm, out_ref,
    wg, wu, wd, gx, gy, stage, xs, ys, part, peer, down, dpeer, dg, du, acc,
    s1, r1, mid, s2, r2,
    w_sem, l_sem, z_send, z_recv, p_send, p_recv, c_send, c_recv, d_send, d_recv,
    a_send, a_recv, b_send, b_recv,
):
    tokens, feats = in_hbm.shape
    rows = nz * tokens
    half = tiles * TILE
    width = feats // CHUNKS
    g = lax.axis_index("groups")
    r = lax.axis_index("row")
    c = lax.axis_index("col")
    x = lax.rem(r, 2)
    z = r // 2
    plane = g * 2 + x

    def z_dev(d):
        return {"row": lax.rem(z + d, nz) * 2 + x}

    def p_index(d):
        return lax.rem(plane + d, 4)

    def p_dev(d):
        q = lax.rem(plane + d, 4)
        return {"groups": q // 2, "row": z * 2 + lax.rem(q, 2)}

    def remote(src, dst, send, recv, device):
        return pltpu.make_async_remote_copy(
            src_ref=src, dst_ref=dst, send_sem=send, recv_sem=recv,
            device_id=device, device_id_type=MESH,
        )

    own = [
        pltpu.make_async_copy(in_hbm, gx.at[plane, z], l_sem.at[0]),
        pltpu.make_async_copy(og_hbm, gy.at[plane, z], l_sem.at[1]),
    ]
    for copy in own:
        copy.start()

    barrier = pltpu.get_barrier_semaphore()
    for d in range(1, nz):
        pl.semaphore_signal(barrier, inc=1, device_id=z_dev(d), device_id_type=MESH)
    for d in range(1, 4):
        pl.semaphore_signal(barrier, inc=1, device_id=p_dev(d), device_id_type=MESH)
    pl.semaphore_signal(barrier, inc=1, device_id={"col": 1 - c}, device_id_type=MESH)

    gates, ups, downs = [], [], []
    for j in range(tiles):
        at = pl.ds(pl.multiple_of(g * half + j * TILE, TILE), TILE)
        to = pl.ds(j * TILE, TILE)
        gates.append(pltpu.make_async_copy(wg_hbm.at[:, at], wg.at[:, to], w_sem.at[0, j]))
        ups.append(pltpu.make_async_copy(wu_hbm.at[:, at], wu.at[:, to], w_sem.at[1, j]))
        downs.append(pltpu.make_async_copy(wd_hbm.at[at, :], wd.at[to, :], w_sem.at[2, j]))
    for j in range(tiles):
        gates[j].start()
        ups[j].start()
    for j in range(tiles):
        downs[j].start()

    for copy in own:
        copy.wait()
    pl.semaphore_wait(barrier, nz + 3)

    buffers = (gx, gy)
    z_copies = [
        [
            remote(buf.at[plane, z], buf.at[plane, z], z_send.at[a, d - 1], z_recv.at[a, d - 1], z_dev(d))
            for d in range(1, nz)
        ]
        for a, buf in enumerate(buffers)
    ]
    p_copies = [
        [
            [
                remote(
                    buf.at[plane, lax.rem(z + nz - k, nz)], buf.at[plane, lax.rem(z + nz - k, nz)],
                    p_send.at[a, k, d - 1], p_recv.at[a, k, d - 1], p_dev(d),
                )
                for d in range(1, 4)
            ]
            for k in range(nz)
        ]
        for a, buf in enumerate(buffers)
    ]
    for copy in z_copies[0] + p_copies[0][0] + z_copies[1]:
        copy.start()
    for a in range(2):
        if a:
            for copy in p_copies[a][0]:
                copy.start()
        for k in range(1, nz):
            z_copies[a][k - 1].wait_recv()
            for copy in p_copies[a][k]:
                copy.start()

    def arrange(a, buf, dst):
        for copies in p_copies[a]:
            for copy in copies:
                copy.wait_recv()
        for q in range(4):
            for k in range(nz):
                at = q * rows + k * tokens
                stage[at:at + tokens, :] = buf[q, k].astype(jnp.float32)
        dst[...] = stage[...].astype(jnp.bfloat16)

    other = {"col": 1 - c}
    gu_moves = [remote(part.at[j], peer.at[j], c_send.at[j], c_recv.at[j], other) for j in range(tiles)]
    dn_moves = [remote(down.at[j], dpeer.at[j], d_send.at[j], d_recv.at[j], other) for j in range(tiles)]

    arrange(0, gx, xs)
    for j in range(tiles):
        cols = slice(j * TILE, (j + 1) * TILE)
        gates[j].wait()
        part[j, 0] = jnp.dot(xs[...], wg[:, cols], preferred_element_type=jnp.float32)
        ups[j].wait()
        part[j, 1] = jnp.dot(xs[...], wu[:, cols], preferred_element_type=jnp.float32)
        gu_moves[j].start()
    arrange(1, gy, ys)
    for j in range(tiles):
        downs[j].wait()
        down[j] = lax.dot_general(
            ys[...], wd[j * TILE:(j + 1) * TILE, :], NT, preferred_element_type=jnp.float32
        )
        dn_moves[j].start()

    def derive(j):
        gu_moves[j].wait_recv()
        dn_moves[j].wait_recv()
        gated = part[j, 0] + peer[j, 0]
        upward = part[j, 1] + peer[j, 1]
        backward = down[j] + dpeer[j]
        sigma = 1.0 / (1.0 + jnp.exp(-gated))
        cols = slice(j * TILE, (j + 1) * TILE)
        dg[:, cols] = (backward * upward * sigma * (1.0 + gated * (1.0 - sigma))).astype(jnp.bfloat16)
        du[:, cols] = (backward * gated * sigma).astype(jnp.bfloat16)

    def product(f, lo, hi):
        at = slice(f * width, (f + 1) * width)
        cols = slice(lo * TILE, hi * TILE)
        return lax.dot_general(
            dg[:, cols], wg[at, cols], NT, preferred_element_type=jnp.float32
        ) + lax.dot_general(du[:, cols], wu[at, cols], NT, preferred_element_type=jnp.float32)

    a_copies = [
        [
            remote(s1.at[f, p_index(d)], r1.at[f, d - 1], a_send.at[f, d - 1], a_recv.at[f, d - 1], p_dev(d))
            for d in range(1, 4)
        ]
        for f in range(CHUNKS)
    ]
    b_copies = [
        [
            remote(s2.at[f, lax.rem(z + d, nz)], r2.at[f, d - 1], b_send.at[f, d - 1], b_recv.at[f, d - 1], z_dev(d))
            for d in range(1, nz)
        ]
        for f in range(CHUNKS)
    ]

    def send_plane(f):
        at = slice(f * width, (f + 1) * width)
        for q in range(4):
            s1[f, q] = acc[q * rows:(q + 1) * rows, at].astype(jnp.bfloat16)
        for copy in a_copies[f]:
            copy.start()

    def send_z(f):
        at = slice(f * width, (f + 1) * width)
        total = acc[pl.ds(pl.multiple_of(plane * rows, rows), rows), at]
        for d in range(1, 4):
            a_copies[f][d - 1].wait_recv()
            total = total + r1[f, d - 1].astype(jnp.float32)
        stage[0:rows, at] = total
        for k in range(nz):
            mid[f, k] = stage[k * tokens:(k + 1) * tokens, at]
            s2[f, k] = mid[f, k].astype(jnp.bfloat16)
        for copy in b_copies[f]:
            copy.start()

    def store(f):
        at = slice(f * width, (f + 1) * width)
        total = mid[f, z]
        for d in range(1, nz):
            b_copies[f][d - 1].wait_recv()
            total = total + r2[f, d - 1].astype(jnp.float32)
        out_ref[:, at] = gx[plane, z, :, at].astype(jnp.float32) * total

    for j in range(tiles - 1):
        derive(j)
    acc[:, 0:width] = product(0, 0, tiles - 1)
    derive(tiles - 1)
    acc[:, 0:width] += product(0, tiles - 1, tiles)
    send_plane(0)
    for f in range(1, CHUNKS):
        acc[:, f * width:(f + 1) * width] = product(f, 0, tiles)
        send_plane(f)
        send_z(f - 1)
        if f > 1:
            store(f - 2)
    send_z(CHUNKS - 1)
    store(CHUNKS - 2)
    store(CHUNKS - 1)

    for copies in z_copies + p_copies[0] + p_copies[1] + [gu_moves, dn_moves] + a_copies + b_copies:
        for copy in copies:
            copy.wait_send()


def shared(nz, inputs, out_grads, w_gate, w_up, w_down):
    tokens, feats = inputs.shape
    half = w_gate.shape[1] // 2
    tiles = half // TILE
    width = feats // CHUNKS
    rows = nz * tokens
    every = 4 * rows
    f32, bf16 = jnp.float32, jnp.bfloat16
    dma = pltpu.SemaphoreType.DMA
    return pl.pallas_call(
        functools.partial(kernel, nz, tiles),
        out_shape=jax.ShapeDtypeStruct((tokens, feats), f32),
        in_specs=[pl.BlockSpec(memory_space=pl.ANY)] * 5,
        out_specs=pl.BlockSpec(memory_space=pltpu.VMEM),
        scratch_shapes=[
            pltpu.VMEM((feats, half), bf16),
            pltpu.VMEM((feats, half), bf16),
            pltpu.VMEM((half, feats), bf16),
            pltpu.VMEM((4, nz, tokens, feats), bf16),
            pltpu.VMEM((4, nz, tokens, feats), bf16),
            pltpu.VMEM((every, feats), f32),
            pltpu.VMEM((every, feats), bf16),
            pltpu.VMEM((every, feats), bf16),
            pltpu.VMEM((tiles, 2, every, TILE), f32),
            pltpu.VMEM((tiles, 2, every, TILE), f32),
            pltpu.VMEM((tiles, every, TILE), f32),
            pltpu.VMEM((tiles, every, TILE), f32),
            pltpu.VMEM((every, half), bf16),
            pltpu.VMEM((every, half), bf16),
            pltpu.VMEM((every, feats), f32),
            pltpu.VMEM((CHUNKS, 4, rows, width), bf16),
            pltpu.VMEM((CHUNKS, 3, rows, width), bf16),
            pltpu.VMEM((CHUNKS, nz, tokens, width), f32),
            pltpu.VMEM((CHUNKS, nz, tokens, width), bf16),
            pltpu.VMEM((CHUNKS, nz - 1, tokens, width), bf16),
            dma((3, tiles)), dma((2,)),
            dma((2, nz - 1)), dma((2, nz - 1)),
            dma((2, nz, 3)), dma((2, nz, 3)),
            dma((tiles,)), dma((tiles,)),
            dma((tiles,)), dma((tiles,)),
            dma((CHUNKS, 3)), dma((CHUNKS, 3)),
            dma((CHUNKS, nz - 1)), dma((CHUNKS, nz - 1)),
        ],
        compiler_params=pltpu.CompilerParams(
            collective_id=0, has_side_effects=True, vmem_limit_bytes=60 << 20
        ),
    )(inputs, out_grads, w_gate, w_up, w_down)


def solution(mesh):
    in_specs = (
        P(("groups", "row"), "col"),
        P(("groups", "row"), "col"),
        P("col", "row"),
        P("col", "row"),
        P("row", "col"),
    )
    out_specs = P(("groups", "row"), "col")
    groups, row, col = (mesh.shape[name] for name in ("groups", "row", "col"))

    def body(inputs, out_grads, w_gate, w_up, w_down):
        tokens, feats = inputs.shape
        nz = row // 2
        hidden = w_gate.shape[1]
        held = 3 * feats * hidden + 60 * groups * row * tokens * feats
        fits = (
            groups == 2 and col == 2 and row % 2 == 0 and nz > 1
            and hidden % (2 * TILE) == 0 and feats % (128 * CHUNKS) == 0 and hidden > 2 * TILE
            and nz * tokens == 8 and held < (56 << 20)
        )
        plan = functools.partial(shared, nz) if fits else per_device
        return plan(inputs, out_grads, w_gate, w_up, w_down)

    return jax.shard_map(
        body, mesh=mesh, in_specs=in_specs, out_specs=out_specs, check_vma=False
    )
```
